1024 devices in a mesh: region: 32 (over y, x_hi, core), member: 32 (over x_lo, z).
Axes of the slice: x: 8 (x_hi: 2, x_lo: 4; x = x_hi * 4 + x_lo), y: 8, z: 8, core: 2. Of those that a mesh axis runs over, the one named last changes fastest.
Arguments:
- ens_obs: bfloat16 [2048, 256, 2048], P('region', 'member'), may hold values from -6 to 6
- ens_state: bfloat16 [2048, 256, 512], P('region', 'member'), may hold values from -6 to 6
- innovation: float32 [2048, 2048], P('region'), may hold values from -6 to 6
- obs_precision: float32 [2048, 2048], P('region'), may hold values from 0.25 to 4
- obs_count: int32 [2048], P('region'), may hold values from 1 to 1920, as said below
Outputs:
- analysis: bfloat16 [2048, 256, 512], P('region', 'member')
The draws below stay inside these ranges and needn't reach their ends.
Inputs may be any that keep to these rules, and one draw needn't show every extreme that they name: Tile t uses its first obs_count[t] observation slots. Over every aligned run of 2 tiles, the numbers of 128-slot blocks that hold used slots, ceil(obs_count / 128), sum to at most 16, and to exactly 16 in one run of every aligned four runs.
All inputs are finite; a program needn't handle non-finite values.
Results may differ from the reference program's by a relative error of at most 0.0057.
Values may be sent and summed in bfloat16 or wider, within the bound.
No kernel may reach another device: no remote copies, remote signals or barrier semaphores. Data moves between devices by JAX's collectives and lax.ppermute only.
A program may use at most 32 MiB of HBM per device.

```python
import math
import jax
import jax.numpy as jnp
from jax import lax

ENS = 256
TILE_VARS = 512
OBS_MAX = 2048
TILE_DEV = 2
NS_ITERS = 4
TILES = 2048
LIVE_BLOCKS = 16


def draw_obs_count(key, part):
    keys = jax.random.split(jax.random.fold_in(key, 17), 4)
    block_full = OBS_MAX // 128
    run_total = TILES // TILE_DEV
    slot_total = TILE_DEV * block_full
    chosen = jax.random.randint(keys[0], (run_total // 4,), 0, 4, dtype=jnp.int32)
    run_index = jnp.arange(run_total, dtype=jnp.int32)
    full_run = run_index % 4 == jnp.repeat(chosen, 4)
    drawn = jax.random.randint(keys[1], (run_total,), TILE_DEV, LIVE_BLOCKS + 1, dtype=jnp.int32)
    budget = jnp.where(full_run, jnp.int32(LIVE_BLOCKS), drawn)
    scores = jax.random.randint(keys[2], (run_total, slot_total), 0, 1048576, dtype=jnp.int32)
    slot_index = jnp.arange(slot_total, dtype=jnp.int32)
    first_tile = slot_index < block_full
    scores = jnp.where(full_run[:, None] & first_tile[None, :], jnp.int32(0), scores)
    leading = slot_index % block_full == 0
    keyed = jnp.where(leading, jnp.int32(0), scores + 1) * slot_total + slot_index
    ordering = jnp.argsort(keyed, axis=1, stable=True).astype(jnp.int32)
    ranking = jnp.argsort(ordering, axis=1, stable=True).astype(jnp.int32)
    picked = (ranking < budget[:, None]).astype(jnp.int32)
    blocks_used = jnp.sum(picked.reshape(run_total, TILE_DEV, block_full), axis=2).astype(jnp.int32)
    missing = jax.random.randint(keys[3], (run_total, TILE_DEV), 0, 128, dtype=jnp.int32)
    tile_index = jnp.arange(TILE_DEV, dtype=jnp.int32)
    missing = jnp.where(full_run[:, None] & (tile_index[None, :] == 0), jnp.int32(0), missing)
    return (blocks_used * 128 - missing).reshape(TILES).astype(jnp.int32)


def level_of(stream_key, shape, shards, least, top_value):
    def one(axis_at, parts):
        draws = jax.random.uniform(jax.random.fold_in(jax.random.fold_in(stream_key, 6), axis_at), (parts,), jnp.float32, least / len(shards), top_value / len(shards))
        return jnp.repeat(jnp.exp(draws), shape[axis_at] // parts).reshape((-1,) + (1,) * (len(shape) - axis_at - 1))

    factor_of = one(*shards[0])
    for cut in shards[1:]:
        factor_of = factor_of * one(*cut)
    return factor_of


def bell_draw(stream_key, shape, scale, reach, cuts=(), kind=jnp.bfloat16):
    factor_of = level_of(stream_key, shape, cuts, -0.22, 0.18) if cuts else 1.0
    values = jax.random.normal(stream_key, shape, jnp.float32) * scale * factor_of
    return jnp.minimum(jnp.maximum(values, -reach), reach).astype(kind)


def setup_inputs(seed: int = 0) -> dict:
    streams_of = jax.random.split(jax.random.key(seed), 6)
    ens_obs = bell_draw(streams_of[0], (TILES, ENS, OBS_MAX), 1.0, 6.0, ((0, 32), (1, 32)))
    ens_state = bell_draw(streams_of[1], (TILES, ENS, TILE_VARS), 1.0, 6.0, ((0, 32), (1, 32)))
    innovation = bell_draw(streams_of[2], (TILES, OBS_MAX), 1.0, 6.0, ((0, 32),), jnp.float32)
    obs_precision = jnp.clip(jnp.exp(math.log(4.0) - 2.7725887 * jax.random.uniform(streams_of[3], (TILES, OBS_MAX), jnp.float32) ** level_of(streams_of[3], (TILES, OBS_MAX), ((0, 32),), -0.2, 0.2)), 0.25, 4.0)
    obs_count = draw_obs_count(jax.random.fold_in(streams_of[5], 71), 0)
    return dict(ens_obs=ens_obs, ens_state=ens_state, innovation=innovation, obs_precision=obs_precision, obs_count=obs_count)


def product(left, right):
    return jnp.dot(left, right, precision=lax.Precision.HIGHEST)

def solve_weights(gram_matrix, obs_drive):
    members = gram_matrix.shape[0]
    identity = jnp.eye(members, dtype=jnp.float32)
    system = gram_matrix + (members - 1.0) * identity
    frobenius = jnp.sqrt(jnp.sum(system * system) + 1e-06)
    root_iter = system / frobenius
    inv_root = identity
    for sweep in range(NS_ITERS):
        factor = 1.5 * identity - 0.5 * product(inv_root, root_iter)
        root_iter = product(root_iter, factor)
        inv_root = product(factor, inv_root)
    inverse = product(inv_root, inv_root) / frobenius
    mean_shift = product(inverse, obs_drive)
    root_part = inv_root * jnp.sqrt((members - 1.0) / frobenius)
    return (mean_shift[:, None] + root_part).astype(jnp.bfloat16)

def transform_tile(state, weights):
    members = state.shape[0]
    average = lax.optimization_barrier(jnp.sum(state, axis=0, dtype=jnp.float32)) / members
    deviation = (state.astype(jnp.float32) - average).astype(jnp.bfloat16)
    moved = lax.dot_general(weights, deviation, (((0,), (0,)), ((), ())), preferred_element_type=jnp.float32)
    return (average + moved).astype(jnp.bfloat16)

def analyse(packed):
    observed, state, innov, precision, live_count = packed
    columns = jnp.arange(observed.shape[1], dtype=jnp.int32)
    weight = jnp.where(columns < live_count, precision, jnp.float32(0.0))
    scaled = (observed.astype(jnp.float32) * weight).astype(jnp.bfloat16)
    gram_matrix = lax.dot_general(scaled, observed, (((1,), (1,)), ((), ())), preferred_element_type=jnp.float32)
    obs_drive = product(observed.astype(jnp.float32), weight * innov)
    return transform_tile(state, solve_weights(gram_matrix, obs_drive))

def reference(ens_obs, ens_state, innovation, obs_precision, obs_count):
    return lax.map(analyse, (ens_obs, ens_state, innovation, obs_precision, obs_count))
```

```python
import jax
import jax.numpy as jnp
from jax import lax
from jax.experimental import pallas as pl
from jax.experimental.pallas import tpu as pltpu
from jax.sharding import PartitionSpec as P

BLOCK = 128
LIVE = 16
SWEEPS = 4
F32, BF16 = jnp.float32, jnp.bfloat16
LAST = (((1,), (1,)), ((), ()))


def pack_kernel(count_ref, obs_ref, state_ref, out_ref, obs_sem, state_sem):
    pairs = out_ref.shape[0]
    state_copy = pltpu.make_async_copy(state_ref, out_ref.at[:, LIVE:], state_sem)
    state_copy.start()

    def start(pair, carry):
        first = lax.shift_right_logical(count_ref[2 * pair] + (BLOCK - 1), 7)
        rest = LIVE - first
        pltpu.make_async_copy(
            obs_ref.at[2 * pair, pl.ds(0, first)], out_ref.at[pair, pl.ds(0, first)], obs_sem
        ).start()
        pltpu.make_async_copy(
            obs_ref.at[2 * pair + 1, pl.ds(0, rest)], out_ref.at[pair, pl.ds(first, rest)], obs_sem
        ).start()
        return carry

    lax.fori_loop(0, pairs, start, 0)
    whole = out_ref.at[:, :LIVE]
    pltpu.make_async_copy(whole, whole, obs_sem).wait()
    state_copy.wait()


def pack(obs_count, ens_obs, ens_state):
    tiles, members, slots = ens_obs.shape
    width = ens_state.shape[2]
    pairs = tiles // 2
    blocks = lambda x, n: x.reshape(tiles, members, n, BLOCK).transpose(0, 2, 1, 3)
    obs = blocks(ens_obs, slots // BLOCK)
    state = blocks(ens_state, width // BLOCK).reshape(pairs, 2 * width // BLOCK, members, BLOCK)
    return pl.pallas_call(
        pack_kernel,
        out_shape=jax.ShapeDtypeStruct((pairs, LIVE + state.shape[1], members, BLOCK), BF16),
        in_specs=[
            pl.BlockSpec(memory_space=pltpu.SMEM),
            pl.BlockSpec(memory_space=pl.ANY),
            pl.BlockSpec(memory_space=pl.ANY),
        ],
        out_specs=pl.BlockSpec(memory_space=pltpu.VMEM),
        scratch_shapes=[pltpu.SemaphoreType.DMA, pltpu.SemaphoreType.DMA],
        name="pack",
    )(obs_count, obs, state)


def split(x):
    high = x.astype(BF16)
    return high, (x - high.astype(F32)).astype(BF16)


def mm(a, b):
    return jnp.dot(a, b, preferred_element_type=F32)


def thirds(x):
    high = x.astype(BF16)
    left = x - high.astype(F32)
    middle = left.astype(BF16)
    low = (left - middle.astype(F32)).astype(BF16)
    return jnp.concatenate([high.astype(F32), middle.astype(F32), low.astype(F32)], axis=0)


def row_times(row, high, low):
    parts = thirds(row)
    lhs = jnp.concatenate([parts, jnp.zeros((5, row.shape[1]), F32)], axis=0).astype(BF16)
    return jnp.sum(mm(lhs, high) + mm(lhs, low), axis=0, keepdims=True)


def analyse_kernel(rank_ref, count_ref, got_ref, innov_ref, prec_ref, out_ref,
                   obs_ref, scaled_ref, line_ref, dev_ref):
    sources, _, each, _ = got_ref.shape
    members = sources * each
    slots = LIVE * BLOCK
    rank = rank_ref[0]
    row = 2 * lax.rem(rank, 4)
    first_blocks = lax.shift_right_logical(count_ref[2 * rank] + (BLOCK - 1), 7)
    column = lax.broadcasted_iota(jnp.int32, (1, slots), 1)

    line_ref[...] = jnp.zeros_like(line_ref)
    for tile in range(2):
        live = column < count_ref[2 * rank + tile]
        weight = jnp.where(live, prec_ref[pl.ds(row + tile, 1), :], 0.0)
        pushed = weight * innov_ref[pl.ds(row + tile, 1), :]
        start = 0 if tile == 0 else pl.multiple_of(first_blocks * BLOCK, BLOCK)
        line_ref[pl.ds(tile, 1), pl.ds(start, slots)] = weight
        line_ref[pl.ds(2 + tile, 1), pl.ds(start, slots)] = pushed

    for block in range(LIVE):
        at = slice(block * BLOCK, (block + 1) * BLOCK)
        values = got_ref[:, block].astype(F32).reshape(members, BLOCK)
        obs_ref[:, at] = values.astype(BF16)
        for tile in range(2):
            scaled_ref[tile, :, at] = (values * line_ref[pl.ds(tile, 1), at]).astype(BF16)

    observed = obs_ref[...]
    lines = jnp.concatenate(
        [thirds(line_ref[pl.ds(2, 1), :slots]), thirds(line_ref[pl.ds(3, 1), :slots]),
         jnp.zeros((2, slots), F32)], axis=0).astype(BF16)
    drives = lax.dot_general(lines, observed, LAST, preferred_element_type=F32)
    drive = [jnp.sum(drives[3 * t:3 * t + 3], axis=0, keepdims=True) for t in range(2)]

    on_diagonal = (lax.broadcasted_iota(jnp.int32, (members, members), 0)
                   == lax.broadcasted_iota(jnp.int32, (members, members), 1))
    eye = jnp.where(on_diagonal, 1.0, 0.0).astype(F32)
    error, root, frob = [], [], []
    for tile in range(2):
        system = lax.dot_general(observed, scaled_ref[tile], LAST, preferred_element_type=F32)
        system = system + (members - 1.0) * eye
        norm = jnp.sqrt(jnp.sum(system * system, keepdims=True) + 1e-06)
        frob.append(norm)
        error.append(system / norm)
        root.append(1.5 * eye - 0.5 * error[tile])

    for sweep in range(1, SWEEPS):
        for tile in range(2):
            e = error[tile]
            e16 = e.astype(BF16)
            g = 1.5 * e - 0.5 * mm(e16, e16)
            e = 1.5 * g - 0.5 * mm(g.astype(BF16), e16)
            error[tile] = e
            z = root[tile]
            root[tile] = 1.5 * z - 0.5 * mm(z.astype(BF16), e.astype(BF16))

    width = out_ref.shape[1] // 2
    for tile in range(2):
        z = root[tile]
        high, low = split(z)
        shift = row_times(row_times(drive[tile], high, low), high, low) / frob[tile]
        transform = (shift + z * jnp.sqrt((members - 1.0) / frob[tile])).astype(BF16)
        averages = []
        for q in range(width):
            state = got_ref[:, LIVE + tile * width + q].astype(F32).reshape(members, BLOCK)
            average = jnp.sum(state, axis=0, keepdims=True) * (1.0 / members)
            averages.append(average)
            dev_ref[:, q * BLOCK:(q + 1) * BLOCK] = (state - average).astype(BF16)
        moved = mm(transform, dev_ref[...])
        for q in range(width):
            result = averages[q] + moved[:, q * BLOCK:(q + 1) * BLOCK]
            out_ref[:, tile * width + q] = result.reshape(sources, each, BLOCK).astype(BF16)


def analyse(rank, obs_count, got, innovation, obs_precision):
    sources, blocks, each, _ = got.shape
    members = sources * each
    slots = innovation.shape[1]
    width = blocks - LIVE
    whole = lambda shape: pl.BlockSpec(shape, lambda i, rank, count: (0,) * len(shape))
    rows = pl.BlockSpec((8, slots), lambda i, rank, count: (lax.div(rank[0], 4), 0))
    return pl.pallas_call(
        analyse_kernel,
        out_shape=jax.ShapeDtypeStruct((sources, width, each, BLOCK), BF16),
        grid_spec=pltpu.PrefetchScalarGridSpec(
            num_scalar_prefetch=2,
            grid=(1,),
            in_specs=[whole(got.shape), rows, rows],
            out_specs=whole((sources, width, each, BLOCK)),
            scratch_shapes=[
                pltpu.VMEM((members, slots), BF16),
                pltpu.VMEM((2, members, slots), BF16),
                pltpu.VMEM((8, 2 * slots), F32),
                pltpu.VMEM((members, width * BLOCK // 2), BF16),
            ],
        ),
        name="analyse",
    )(rank, obs_count, got, innovation, obs_precision)


def local(ens_obs, ens_state, innovation, obs_precision, obs_count):
    tiles, each, variables = ens_state.shape
    rank = lax.axis_index("member").astype(jnp.int32).reshape(1)
    exchange = lambda x: lax.all_to_all(x, "member", split_axis=0, concat_axis=0, tiled=True)
    got = exchange(pack(obs_count, ens_obs, ens_state))
    back = exchange(analyse(rank, obs_count, got, innovation, obs_precision))
    back = back.reshape(tiles, variables // BLOCK, each, BLOCK)
    return back.transpose(0, 2, 1, 3).reshape(tiles, each, variables)


def solution(mesh):
    placed = (
        P("region", "member", None),
        P("region", "member", None),
        P("region", None),
        P("region", None),
        P("region"),
    )
    return jax.shard_map(
        local, mesh=mesh, in_specs=placed, out_specs=P("region", "member", None), check_vma=False
    )
```

```python
import jax
import jax.numpy as jnp
from jax import lax
from jax.experimental import pallas as pl
from jax.experimental.pallas import tpu as pltpu
from jax.sharding import PartitionSpec as P

BLOCK = 128
LIVE = 16
F32, BF16 = jnp.float32, jnp.bfloat16
LAST = (((1,), (1,)), ((), ()))


def pack_kernel(count_ref, obs_ref, state_ref, out_ref, obs_sem, state_sem):
    pairs = out_ref.shape[0]
    state_copy = pltpu.make_async_copy(state_ref, out_ref.at[:, LIVE:], state_sem)
    state_copy.start()

    def start(pair, carry):
        first = lax.shift_right_logical(count_ref[2 * pair] + (BLOCK - 1), 7)
        rest = LIVE - first
        pltpu.make_async_copy(
            obs_ref.at[2 * pair, pl.ds(0, first)], out_ref.at[pair, pl.ds(0, first)], obs_sem
        ).start()
        pltpu.make_async_copy(
            obs_ref.at[2 * pair + 1, pl.ds(0, rest)], out_ref.at[pair, pl.ds(first, rest)], obs_sem
        ).start()
        return carry

    lax.fori_loop(0, pairs, start, 0)
    whole = out_ref.at[:, :LIVE]
    pltpu.make_async_copy(whole, whole, obs_sem).wait()
    state_copy.wait()


def pack(obs_count, ens_obs, ens_state):
    tiles, members, slots = ens_obs.shape
    width = ens_state.shape[2]
    pairs = tiles // 2
    blocks = lambda x, n: x.reshape(tiles, members, n, BLOCK).transpose(0, 2, 1, 3)
    obs = blocks(ens_obs, slots // BLOCK)
    state = blocks(ens_state, width // BLOCK).reshape(pairs, 2 * width // BLOCK, members, BLOCK)
    return pl.pallas_call(
        pack_kernel,
        out_shape=pltpu.VMEM((pairs, LIVE + state.shape[1], members, BLOCK), BF16),
        in_specs=[
            pl.BlockSpec(memory_space=pltpu.SMEM),
            pl.BlockSpec(memory_space=pl.ANY),
            pl.BlockSpec(memory_space=pl.ANY),
        ],
        out_specs=pl.BlockSpec(memory_space=pltpu.VMEM),
        scratch_shapes=[pltpu.SemaphoreType.DMA, pltpu.SemaphoreType.DMA],
        name="pack",
    )(obs_count, obs, state)


def mm(a, b):
    return jnp.dot(a.astype(BF16), b.astype(BF16), preferred_element_type=F32)


def thirds(x):
    high = x.astype(BF16).astype(F32)
    middle = (x - high).astype(BF16).astype(F32)
    return [high, middle, x - high - middle]


C0, C1, C2, C3, C4 = 2.25, -2.4375, 1.6875, -0.5625, 0.0625


def analyse_kernel(rank_ref, count_ref, got_ref, innov_ref, prec_ref, out_ref, line_ref):
    sources, blocks, each, _ = got_ref.shape
    members = sources * each
    slots = LIVE * BLOCK
    width = (blocks - LIVE) // 2
    rank = rank_ref[0]
    row = 2 * lax.rem(rank, 4)
    first_slots = pl.multiple_of(
        lax.shift_right_logical(count_ref[2 * rank] + (BLOCK - 1), 7) * BLOCK, BLOCK)
    column = lax.broadcasted_iota(jnp.int32, (1, slots), 1)

    line_ref[...] = jnp.zeros_like(line_ref)
    for tile in range(2):
        live = column < count_ref[2 * rank + tile]
        weight = jnp.where(live, prec_ref[pl.ds(row + tile, 1), :], 0.0)
        pushed = weight * innov_ref[pl.ds(row + tile, 1), :]
        start = 0 if tile == 0 else first_slots
        line_ref[pl.ds(tile, 1), pl.ds(start, slots)] = weight
        line_ref[pl.ds(2 + tile, 1), pl.ds(start, slots)] = pushed

    weights = [line_ref[pl.ds(t, 1), :slots] for t in range(2)]
    parts = thirds(line_ref[pl.ds(2, 1), :slots]) + thirds(line_ref[pl.ds(3, 1), :slots])
    pushes = jnp.concatenate(parts + [jnp.zeros((10, slots), F32)], axis=0).astype(BF16)

    observed, scaled = [], [[], []]
    for block in range(LIVE):
        at = slice(block * BLOCK, (block + 1) * BLOCK)
        values = got_ref[:, block].reshape(members, BLOCK)
        observed.append(values)
        for tile in range(2):
            scaled[tile].append((values.astype(F32) * weights[tile][:, at]).astype(BF16))
    observed = jnp.concatenate(observed, axis=1)
    left = jnp.concatenate(
        [jnp.concatenate(scaled[0], axis=1), jnp.concatenate(scaled[1], axis=1), pushes], axis=0)
    sums = lax.dot_general(left, observed, LAST, preferred_element_type=F32)
    drives = sums[2 * members:]
    drive = [jnp.sum(drives[3 * t:3 * t + 3], axis=0, keepdims=True) for t in range(2)]

    on_diagonal = (lax.broadcasted_iota(jnp.int32, (members, members), 0)
                   == lax.broadcasted_iota(jnp.int32, (members, members), 1))
    unit, frob = [], []
    for t in range(2):
        system = sums[t * members:(t + 1) * members]
        system = jnp.where(on_diagonal, system + (members - 1.0), system)
        norm = jnp.sqrt(jnp.sum(system * system, keepdims=True) + 1e-06)
        frob.append(norm)
        unit.append(system / norm)

    def sweeps(e):
        square = [mm(x, x) for x in e]
        tail = [mm(q, C3 * x + C4 * q) for q, x in zip(square, e)]
        return [C1 * x + C2 * q + r for x, q, r in zip(e, square, tail)]

    first = sweeps(unit)
    moved_y = [C0 * x + mm(x, d) for x, d in zip(unit, first)]
    second = sweeps([C0 * y + mm(y, d) for y, d in zip(moved_y, first)])
    rest = [C0 * (d + q) + mm(d, q) for d, q in zip(first, second)]

    averages, deviations = [[], []], [[], []]
    for t in range(2):
        for q in range(width):
            state = got_ref[:, LIVE + t * width + q].reshape(members, BLOCK).astype(F32)
            average = jnp.sum(state, axis=0, keepdims=True) * (1.0 / members)
            averages[t].append(average)
            deviations[t].append((state - average).astype(BF16))

    for t in range(2):
        root = jnp.where(on_diagonal, rest[t] + C0 * C0, rest[t])
        once = jnp.sum(root * drive[t], axis=1, keepdims=True)
        shift = jnp.sum(root * once, axis=0, keepdims=True) / frob[t]
        scale = jnp.sqrt((members - 1.0) / frob[t])
        transform = (shift + root * scale).astype(BF16)
        moved = mm(transform, jnp.concatenate(deviations[t], axis=1))
        for q in range(width):
            result = averages[t][q] + moved[:, q * BLOCK:(q + 1) * BLOCK]
            out_ref[:, t * width + q] = result.astype(BF16).reshape(sources, each, BLOCK)


def analyse(rank, obs_count, got, innovation, obs_precision):
    sources, blocks, each, _ = got.shape
    slots = innovation.shape[1]
    rows = pl.BlockSpec((8, slots), lambda i, rank, count: (lax.div(rank[0], 4), 0))
    vmem = pl.BlockSpec(memory_space=pltpu.VMEM)
    return pl.pallas_call(
        analyse_kernel,
        out_shape=pltpu.VMEM((sources, blocks - LIVE, each, BLOCK), BF16),
        grid_spec=pltpu.PrefetchScalarGridSpec(
            num_scalar_prefetch=2,
            grid=(1,),
            in_specs=[vmem, rows, rows],
            out_specs=vmem,
            scratch_shapes=[pltpu.VMEM((8, 2 * slots), F32)],
        ),
        name="analyse",
    )(rank, obs_count, pltpu.with_memory_space_constraint(got, pltpu.VMEM), innovation, obs_precision)


def local(ens_obs, ens_state, innovation, obs_precision, obs_count):
    tiles, each, variables = ens_state.shape
    rank = lax.axis_index("member").astype(jnp.int32).reshape(1)
    exchange = lambda x: lax.all_to_all(x, "member", split_axis=0, concat_axis=0, tiled=True)
    packed, rank = lax.optimization_barrier((pack(obs_count, ens_obs, ens_state), rank))
    got = exchange(packed)
    back = exchange(analyse(rank, obs_count, got, innovation, obs_precision))
    back = back.reshape(tiles, variables // BLOCK, each, BLOCK)
    return back.transpose(0, 2, 1, 3).reshape(tiles, each, variables)


def solution(mesh):
    placed = (
        P("region", "member", None),
        P("region", "member", None),
        P("region", None),
        P("region", None),
        P("region"),
    )
    return jax.shard_map(
        local, mesh=mesh, in_specs=placed, out_specs=P("region", "member", None), check_vma=False
    )
```

```python
import jax
import jax.numpy as jnp
from jax import lax
from jax.experimental import pallas as pl
from jax.experimental.pallas import tpu as pltpu
from jax.sharding import PartitionSpec as P

BLOCK = 128
LIVE = 16
STEP = 4
F32, BF16 = jnp.float32, jnp.bfloat16
LAST = (((1,), (1,)), ((), ()))


def thirds(x):
    high = x.astype(BF16).astype(F32)
    middle = (x - high).astype(BF16).astype(F32)
    return [high, middle, x - high - middle]


def blocks_used(count):
    return lax.shift_right_logical(count + (BLOCK - 1), 7)


def pack_kernel(rank_ref, count_ref, obs_ref, state_ref, innov_ref, prec_ref,
                out_ref, weight_ref, push_ref,
                innov_rows, prec_rows, line_ref, obs_sem, state_sem, innov_sem, prec_sem):
    pairs = out_ref.shape[0]
    slots = LIVE * BLOCK
    rank = rank_ref[0]
    eight = pl.ds(pl.multiple_of(8 * lax.div(rank, 4), 8), 8)
    copies = [
        pltpu.make_async_copy(state_ref, out_ref.at[:, LIVE:], state_sem),
        pltpu.make_async_copy(innov_ref.at[eight], innov_rows, innov_sem),
        pltpu.make_async_copy(prec_ref.at[eight], prec_rows, prec_sem),
    ]
    for copy in copies:
        copy.start()

    def start(pair, carry):
        first = blocks_used(count_ref[2 * pair])
        rest = LIVE - first
        pltpu.make_async_copy(
            obs_ref.at[2 * pair, pl.ds(0, first)], out_ref.at[pair, pl.ds(0, first)], obs_sem
        ).start()
        pltpu.make_async_copy(
            obs_ref.at[2 * pair + 1, pl.ds(0, rest)], out_ref.at[pair, pl.ds(first, rest)], obs_sem
        ).start()
        return carry

    lax.fori_loop(0, pairs, start, 0)

    row = 2 * lax.rem(rank, 4)
    first = blocks_used(count_ref[2 * rank])
    column = lax.broadcasted_iota(jnp.int32, (1, slots), 1)
    line_ref[...] = jnp.zeros_like(line_ref)
    for copy in copies[1:]:
        copy.wait()
    for tile in range(2):
        live = column < count_ref[2 * rank + tile]
        weight = jnp.where(live, prec_rows[pl.ds(row + tile, 1), :], 0.0)
        begin = 0 if tile == 0 else pl.multiple_of(first * BLOCK, BLOCK)
        line_ref[pl.ds(tile, 1), pl.ds(begin, slots)] = weight
        line_ref[pl.ds(2 + tile, 1), pl.ds(begin, slots)] = weight * innov_rows[pl.ds(row + tile, 1), :]
    weight_ref[:2] = line_ref[:2, :slots]
    weight_ref[2:] = jnp.full((6, slots), first.astype(F32))
    parts = thirds(line_ref[pl.ds(2, 1), :slots]) + thirds(line_ref[pl.ds(3, 1), :slots])
    push_ref[...] = jnp.concatenate(parts + [jnp.zeros((10, slots), F32)], axis=0).astype(BF16)

    whole = out_ref.at[:, :LIVE]
    pltpu.make_async_copy(whole, whole, obs_sem).wait()
    copies[0].wait()


def pack(rank, obs_count, ens_obs, ens_state, innovation, obs_precision):
    tiles, members, slots = ens_obs.shape
    width = ens_state.shape[2]
    pairs = tiles // 2
    blocks = lambda x, n: x.reshape(tiles, members, n, BLOCK).transpose(0, 2, 1, 3)
    obs = blocks(ens_obs, slots // BLOCK)
    state = blocks(ens_state, width // BLOCK).reshape(pairs, 2 * width // BLOCK, members, BLOCK)
    smem, hbm, vmem = (pl.BlockSpec(memory_space=m) for m in (pltpu.SMEM, pl.ANY, pltpu.VMEM))
    return pl.pallas_call(
        pack_kernel,
        out_shape=(
            pltpu.VMEM((pairs, LIVE + state.shape[1], members, BLOCK), BF16),
            pltpu.VMEM((8, slots), F32),
            pltpu.VMEM((16, slots), BF16),
        ),
        in_specs=[smem, smem, hbm, hbm, hbm, hbm],
        out_specs=(vmem, vmem, vmem),
        scratch_shapes=[
            pltpu.VMEM((8, slots), F32),
            pltpu.VMEM((8, slots), F32),
            pltpu.VMEM((8, 2 * slots), F32),
        ] + [pltpu.SemaphoreType.DMA] * 4,
        name="pack",
    )(rank, obs_count, obs, state, innovation, obs_precision)


def mm(a, b):
    return jnp.dot(a.astype(BF16), b.astype(BF16), preferred_element_type=F32)


C0, C1, C2, C3, C4 = 2.25, -2.4375, 1.6875, -0.5625, 0.0625


def analyse_kernel(got_ref, weight_ref, push_ref, out_ref, sum_ref):
    sources, blocks, each, _ = got_ref.shape
    members = sources * each
    width = (blocks - LIVE) // 2

    def values_of(block):
        return got_ref[:, block].reshape(members, BLOCK)

    def product(first, last, tiles):
        observed = [values_of(block) for block in range(first, last)]
        at = slice(first * BLOCK, last * BLOCK)
        rows = []
        for tile in tiles:
            rows.append(jnp.concatenate(
                [(x.astype(F32) * weight_ref[pl.ds(tile, 1), pl.ds((first + i) * BLOCK, BLOCK)]).astype(BF16)
                 for i, x in enumerate(observed)], axis=1))
        left = jnp.concatenate(rows + [push_ref[:, at]], axis=0)
        return lax.dot_general(
            left, jnp.concatenate(observed, axis=1), LAST, preferred_element_type=F32)

    stretch = lax.div(jnp.max(weight_ref[pl.ds(2, 1), :BLOCK]).astype(jnp.int32), STEP)
    for part in range(LIVE // STEP):
        low, high = part * STEP, (part + 1) * STEP

        @pl.when(stretch == part)
        def _():
            middle = product(low, high, (0, 1))
            first, second, lines = middle[:members], middle[members:2 * members], middle[2 * members:]
            if low:
                more = product(0, low, (0,))
                first, lines = first + more[:members], lines + more[members:]
            if high < LIVE:
                more = product(high, LIVE, (1,))
                second, lines = second + more[:members], lines + more[members:]
            sum_ref[:members] = first
            sum_ref[members:2 * members] = second
            sum_ref[2 * members:] = lines

    drives = sum_ref[2 * members:]
    drive = [jnp.sum(drives[3 * t:3 * t + 3], axis=0, keepdims=True) for t in range(2)]

    averages, deviations = [[], []], [[], []]
    waiting = [(t, q) for t in range(2) for q in range(width)]

    def prepare(count):
        for t, q in waiting[:count]:
            state = values_of(LIVE + t * width + q).astype(F32)
            average = jnp.sum(state, axis=0, keepdims=True) * (1.0 / members)
            averages[t].append(average)
            deviations[t].append((state - average).astype(BF16))
        del waiting[:count]

    on_diagonal = (lax.broadcasted_iota(jnp.int32, (members, members), 0)
                   == lax.broadcasted_iota(jnp.int32, (members, members), 1))
    unit, square, frob = [], [], []
    for t in range(2):
        system = sum_ref[t * members:(t + 1) * members]
        system = jnp.where(on_diagonal, system + (members - 1.0), system)
        raw = mm(system, system)
        norm = jnp.sqrt(jnp.sum(system * system, keepdims=True) + 1e-06)
        inverse = 1.0 / norm
        frob.append(norm)
        unit.append(system * inverse)
        square.append(raw * (inverse * inverse))
    prepare(2)

    def sweeps(e, square):
        tail = [mm(q, C3 * x + C4 * q) for q, x in zip(square, e)]
        return [C1 * x + C2 * q + r for x, q, r in zip(e, square, tail)]

    first = sweeps(unit, square)
    prepare(2)
    moved_y = [C0 * x + mm(x, d) for x, d in zip(unit, first)]
    prepare(2)
    error = [C0 * y + mm(y, d) for y, d in zip(moved_y, first)]
    prepare(2)
    second = sweeps(error, [mm(x, x) for x in error])
    rest = [C0 * (d + q) + mm(d, q) for d, q in zip(first, second)]

    for t in range(2):
        root = jnp.where(on_diagonal, rest[t] + C0 * C0, rest[t])
        once = jnp.sum(root * drive[t], axis=1, keepdims=True)
        shift = jnp.sum(root * once, axis=0, keepdims=True) / frob[t]
        scale = jnp.sqrt((members - 1.0) / frob[t])
        transform = (shift + root * scale).astype(BF16)
        moved = mm(transform, jnp.concatenate(deviations[t], axis=1))
        for q in range(width):
            result = averages[t][q] + moved[:, q * BLOCK:(q + 1) * BLOCK]
            out_ref[:, t * width + q] = result.astype(BF16).reshape(sources, each, BLOCK)


def analyse(got, weights, pushes):
    sources, blocks, each, _ = got.shape
    members = sources * each
    vmem = pl.BlockSpec(memory_space=pltpu.VMEM)
    here = lambda x: pltpu.with_memory_space_constraint(x, pltpu.VMEM)
    return pl.pallas_call(
        analyse_kernel,
        out_shape=pltpu.VMEM((sources, blocks - LIVE, each, BLOCK), BF16),
        in_specs=[vmem, vmem, vmem],
        out_specs=vmem,
        scratch_shapes=[pltpu.VMEM((2 * members + 16, members), F32)],
        name="analyse",
    )(here(got), here(weights), here(pushes))


def local(ens_obs, ens_state, innovation, obs_precision, obs_count):
    tiles, each, variables = ens_state.shape
    rank = lax.axis_index("member").astype(jnp.int32).reshape(1)
    exchange = lambda x: lax.all_to_all(x, "member", split_axis=0, concat_axis=0, tiled=True)
    packed, weights, pushes = pack(
        rank, obs_count, ens_obs, ens_state, innovation, obs_precision)
    back = exchange(analyse(exchange(packed), weights, pushes))
    back = back.reshape(tiles, variables // BLOCK, each, BLOCK)
    return back.transpose(0, 2, 1, 3).reshape(tiles, each, variables)


def solution(mesh):
    placed = (
        P("region", "member", None),
        P("region", "member", None),
        P("region", None),
        P("region", None),
        P("region"),
    )
    return jax.shard_map(
        local, mesh=mesh, in_specs=placed, out_specs=P("region", "member", None), check_vma=False
    )
```

```python
import jax
import jax.numpy as jnp
from jax import lax
from jax.experimental import pallas as pl
from jax.experimental.pallas import tpu as pltpu
from jax.sharding import PartitionSpec as P

BLOCK = 128
LIVE = 16
STEP = 4
F32, BF16 = jnp.float32, jnp.bfloat16
LAST = (((1,), (1,)), ((), ()))


def thirds(x):
    high = x.astype(BF16).astype(F32)
    middle = (x - high).astype(BF16).astype(F32)
    return [high, middle, x - high - middle]


def blocks_used(count):
    return lax.shift_right_logical(count + (BLOCK - 1), 7)


def pack_kernel(rank_ref, count_ref, obs_ref, state_ref, innov_ref, prec_ref,
                out_ref, weight_ref, push_ref,
                innov_rows, prec_rows, line_ref, obs_sem, state_sem, innov_sem, prec_sem):
    pairs = out_ref.shape[0]
    slots = LIVE * BLOCK
    rank = rank_ref[0]
    eight = pl.ds(pl.multiple_of(8 * lax.div(rank, 4), 8), 8)
    copies = [
        pltpu.make_async_copy(state_ref, out_ref.at[:, LIVE:], state_sem),
        pltpu.make_async_copy(innov_ref.at[eight], innov_rows, innov_sem),
        pltpu.make_async_copy(prec_ref.at[eight], prec_rows, prec_sem),
    ]
    for copy in copies:
        copy.start()

    def start(pair, carry):
        first = blocks_used(count_ref[2 * pair])
        rest = LIVE - first
        pltpu.make_async_copy(
            obs_ref.at[2 * pair, pl.ds(0, first)], out_ref.at[pair, pl.ds(0, first)], obs_sem
        ).start()
        pltpu.make_async_copy(
            obs_ref.at[2 * pair + 1, pl.ds(0, rest)], out_ref.at[pair, pl.ds(first, rest)], obs_sem
        ).start()
        return carry

    lax.fori_loop(0, pairs, start, 0)

    row = 2 * lax.rem(rank, 4)
    first = blocks_used(count_ref[2 * rank])
    column = lax.broadcasted_iota(jnp.int32, (1, slots), 1)
    line_ref[...] = jnp.zeros_like(line_ref)
    for copy in copies[1:]:
        copy.wait()
    for tile in range(2):
        live = column < count_ref[2 * rank + tile]
        weight = jnp.where(live, prec_rows[pl.ds(row + tile, 1), :], 0.0)
        begin = 0 if tile == 0 else pl.multiple_of(first * BLOCK, BLOCK)
        line_ref[pl.ds(tile, 1), pl.ds(begin, slots)] = weight
        line_ref[pl.ds(2 + tile, 1), pl.ds(begin, slots)] = weight * innov_rows[pl.ds(row + tile, 1), :]
    weight_ref[:2] = line_ref[:2, :slots]
    weight_ref[2:] = jnp.full((6, slots), first.astype(F32))
    parts = thirds(line_ref[pl.ds(2, 1), :slots]) + thirds(line_ref[pl.ds(3, 1), :slots])
    push_ref[...] = jnp.concatenate(parts + [jnp.zeros((10, slots), F32)], axis=0).astype(BF16)

    whole = out_ref.at[:, :LIVE]
    pltpu.make_async_copy(whole, whole, obs_sem).wait()
    copies[0].wait()


def pack(rank, obs_count, ens_obs, ens_state, innovation, obs_precision):
    tiles, members, slots = ens_obs.shape
    width = ens_state.shape[2]
    pairs = tiles // 2
    blocks = lambda x, n: x.reshape(tiles, members, n, BLOCK).transpose(0, 2, 1, 3)
    obs = blocks(ens_obs, slots // BLOCK)
    state = blocks(ens_state, width // BLOCK).reshape(pairs, 2 * width // BLOCK, members, BLOCK)
    smem, hbm, vmem = (pl.BlockSpec(memory_space=m) for m in (pltpu.SMEM, pl.ANY, pltpu.VMEM))
    return pl.pallas_call(
        pack_kernel,
        out_shape=(
            pltpu.VMEM((pairs, LIVE + state.shape[1], members, BLOCK), BF16),
            pltpu.VMEM((8, slots), F32),
            pltpu.VMEM((16, slots), BF16),
        ),
        in_specs=[smem, smem, hbm, hbm, hbm, hbm],
        out_specs=(vmem, vmem, vmem),
        scratch_shapes=[
            pltpu.VMEM((8, slots), F32),
            pltpu.VMEM((8, slots), F32),
            pltpu.VMEM((8, 2 * slots), F32),
        ] + [pltpu.SemaphoreType.DMA] * 4,
        name="pack",
    )(rank, obs_count, obs, state, innovation, obs_precision)


def mm(a, b):
    return jnp.dot(a.astype(BF16), b.astype(BF16), preferred_element_type=F32)


C0, C1, C2, C3, C4 = 2.25, -2.4375, 1.6875, -0.5625, 0.0625


def analyse_kernel(got_ref, weight_ref, push_ref, out_ref, sum_ref):
    sources, blocks, each, _ = got_ref.shape
    members = sources * each
    width = (blocks - LIVE) // 2

    def values_of(block):
        return got_ref[:, block].reshape(members, BLOCK)

    def product(first, last, tiles):
        observed = [values_of(block) for block in range(first, last)]
        at = slice(first * BLOCK, last * BLOCK)
        rows = []
        for tile in tiles:
            rows.append(jnp.concatenate(
                [(x.astype(F32) * weight_ref[pl.ds(tile, 1), pl.ds((first + i) * BLOCK, BLOCK)]).astype(BF16)
                 for i, x in enumerate(observed)], axis=1))
        left = jnp.concatenate(rows + [push_ref[:, at]], axis=0)
        return lax.dot_general(
            left, jnp.concatenate(observed, axis=1), LAST, preferred_element_type=F32)

    stretch = lax.div(jnp.max(weight_ref[pl.ds(2, 1), :BLOCK]).astype(jnp.int32), STEP)
    for part in range(LIVE // STEP):
        low, high = part * STEP, (part + 1) * STEP

        @pl.when(stretch == part)
        def _():
            middle = product(low, high, (0, 1))
            first, second, lines = middle[:members], middle[members:2 * members], middle[2 * members:]
            if low:
                more = product(0, low, (0,))
                first, lines = first + more[:members], lines + more[members:]
            if high < LIVE:
                more = product(high, LIVE, (1,))
                second, lines = second + more[:members], lines + more[members:]
            sum_ref[:members] = first
            sum_ref[members:2 * members] = second
            sum_ref[2 * members:] = lines

    drives = sum_ref[2 * members:]
    drive = [jnp.sum(drives[3 * t:3 * t + 3], axis=0, keepdims=True) for t in range(2)]

    averages, deviations = [[], []], [[], []]
    waiting = [(t, q) for t in range(2) for q in range(width)]

    def prepare(count):
        for t, q in waiting[:count]:
            state = values_of(LIVE + t * width + q).astype(F32)
            average = jnp.sum(state, axis=0, keepdims=True) * (1.0 / members)
            averages[t].append(average)
            deviations[t].append((state - average).astype(BF16))
        del waiting[:count]

    on_diagonal = (lax.broadcasted_iota(jnp.int32, (members, members), 0)
                   == lax.broadcasted_iota(jnp.int32, (members, members), 1))
    unit, square, frob = [], [], []
    for t in range(2):
        system = sum_ref[t * members:(t + 1) * members]
        system = jnp.where(on_diagonal, system + (members - 1.0), system)
        raw = mm(system, system)
        norm = jnp.sqrt(jnp.sum(system * system, keepdims=True) + 1e-06)
        inverse = 1.0 / norm
        frob.append(norm)
        unit.append(system * inverse)
        square.append(raw * (inverse * inverse))
    prepare(2)

    def sweeps(e, square):
        tail = [mm(C3 * x + C4 * q, q) for q, x in zip(square, e)]
        return [C1 * x + C2 * q + r for x, q, r in zip(e, square, tail)]

    first = sweeps(unit, square)
    prepare(2)
    moved_y = [C0 * x + mm(d, x) for x, d in zip(unit, first)]
    prepare(2)
    error = [C0 * y + mm(y, d) for y, d in zip(moved_y, first)]
    prepare(2)
    second = sweeps(error, [mm(x, x) for x in error])
    rest = [C0 * (d + q) + mm(q, d) for d, q in zip(first, second)]

    for t in range(2):
        root = jnp.where(on_diagonal, rest[t] + C0 * C0, rest[t])
        once = jnp.sum(root * drive[t], axis=1, keepdims=True)
        shift = jnp.sum(root * once, axis=0, keepdims=True) / frob[t]
        scale = jnp.sqrt((members - 1.0) / frob[t])
        transform = (shift + root * scale).astype(BF16)
        moved = mm(transform, jnp.concatenate(deviations[t], axis=1))
        for q in range(width):
            result = averages[t][q] + moved[:, q * BLOCK:(q + 1) * BLOCK]
            out_ref[:, t * width + q] = result.astype(BF16).reshape(sources, each, BLOCK)


def analyse(got, weights, pushes):
    sources, blocks, each, _ = got.shape
    members = sources * each
    vmem = pl.BlockSpec(memory_space=pltpu.VMEM)
    here = lambda x: pltpu.with_memory_space_constraint(x, pltpu.VMEM)
    return pl.pallas_call(
        analyse_kernel,
        out_shape=pltpu.VMEM((sources, blocks - LIVE, each, BLOCK), BF16),
        in_specs=[vmem, vmem, vmem],
        out_specs=vmem,
        scratch_shapes=[pltpu.VMEM((2 * members + 16, members), F32)],
        name="analyse",
    )(here(got), here(weights), here(pushes))


def local(ens_obs, ens_state, innovation, obs_precision, obs_count):
    tiles, each, variables = ens_state.shape
    rank = lax.axis_index("member").astype(jnp.int32).reshape(1)
    exchange = lambda x: lax.all_to_all(x, "member", split_axis=0, concat_axis=0, tiled=True)
    packed, weights, pushes = pack(
        rank, obs_count, ens_obs, ens_state, innovation, obs_precision)
    back = exchange(analyse(exchange(packed), weights, pushes))
    back = back.reshape(tiles, variables // BLOCK, each, BLOCK)
    return back.transpose(0, 2, 1, 3).reshape(tiles, each, variables)


def solution(mesh):
    placed = (
        P("region", "member", None),
        P("region", "member", None),
        P("region", None),
        P("region", None),
        P("region"),
    )
    return jax.shard_map(
        local, mesh=mesh, in_specs=placed, out_specs=P("region", "member", None), check_vma=False
    )
```

```python
import jax
import jax.numpy as jnp
from jax import lax
from jax.experimental import pallas as pl
from jax.experimental.pallas import tpu as pltpu
from jax.sharding import PartitionSpec as P

BLOCK = 128
LIVE = 16
STEP = 4
F32, BF16 = jnp.float32, jnp.bfloat16
LAST = (((1,), (1,)), ((), ()))


def thirds(x):
    high = x.astype(BF16).astype(F32)
    middle = (x - high).astype(BF16).astype(F32)
    return [high, middle, x - high - middle]


def blocks_used(count):
    return lax.shift_right_logical(count + (BLOCK - 1), 7)


def pack_kernel(count_hbm, obs_ref, state_ref, innov_ref, prec_ref,
                out_ref, weight_ref, push_ref,
                count_ref, innov_rows, prec_rows, line_ref,
                count_sem, obs_sem, state_sem, innov_sem, prec_sem):
    pairs = out_ref.shape[0]
    slots = LIVE * BLOCK
    rank = lax.axis_index("member")
    count_copy = pltpu.make_async_copy(count_hbm, count_ref, count_sem)
    count_copy.start()
    eight = pl.ds(pl.multiple_of(8 * lax.div(rank, 4), 8), 8)
    copies = [
        pltpu.make_async_copy(state_ref, out_ref.at[:, LIVE:], state_sem),
        pltpu.make_async_copy(innov_ref.at[eight], innov_rows, innov_sem),
        pltpu.make_async_copy(prec_ref.at[eight], prec_rows, prec_sem),
    ]
    for copy in copies:
        copy.start()
    count_copy.wait()

    def start(pair, carry):
        first = blocks_used(count_ref[2 * pair])
        rest = LIVE - first
        pltpu.make_async_copy(
            obs_ref.at[2 * pair, pl.ds(0, first)], out_ref.at[pair, pl.ds(0, first)], obs_sem
        ).start()
        pltpu.make_async_copy(
            obs_ref.at[2 * pair + 1, pl.ds(0, rest)], out_ref.at[pair, pl.ds(first, rest)], obs_sem
        ).start()
        return carry

    lax.fori_loop(0, pairs, start, 0)

    row = 2 * lax.rem(rank, 4)
    first = blocks_used(count_ref[2 * rank])
    column = lax.broadcasted_iota(jnp.int32, (1, slots), 1)
    line_ref[...] = jnp.zeros_like(line_ref)
    for copy in copies[1:]:
        copy.wait()
    for tile in range(2):
        live = column < count_ref[2 * rank + tile]
        weight = jnp.where(live, prec_rows[pl.ds(row + tile, 1), :], 0.0)
        begin = 0 if tile == 0 else pl.multiple_of(first * BLOCK, BLOCK)
        line_ref[pl.ds(tile, 1), pl.ds(begin, slots)] = weight
        line_ref[pl.ds(2 + tile, 1), pl.ds(begin, slots)] = weight * innov_rows[pl.ds(row + tile, 1), :]
    weight_ref[:2] = line_ref[:2, :slots]
    weight_ref[2:] = jnp.full((6, slots), first.astype(F32))
    parts = thirds(line_ref[pl.ds(2, 1), :slots]) + thirds(line_ref[pl.ds(3, 1), :slots])
    push_ref[...] = jnp.concatenate(parts + [jnp.zeros((10, slots), F32)], axis=0).astype(BF16)

    whole = out_ref.at[:, :LIVE]
    pltpu.make_async_copy(whole, whole, obs_sem).wait()
    copies[0].wait()


def pack(obs_count, ens_obs, ens_state, innovation, obs_precision):
    tiles, members, slots = ens_obs.shape
    width = ens_state.shape[2]
    pairs = tiles // 2
    blocks = lambda x, n: x.reshape(tiles, members, n, BLOCK).transpose(0, 2, 1, 3)
    obs = blocks(ens_obs, slots // BLOCK)
    state = blocks(ens_state, width // BLOCK).reshape(pairs, 2 * width // BLOCK, members, BLOCK)
    hbm, vmem = (pl.BlockSpec(memory_space=m) for m in (pl.ANY, pltpu.VMEM))
    return pl.pallas_call(
        pack_kernel,
        out_shape=(
            pltpu.VMEM((pairs, LIVE + state.shape[1], members, BLOCK), BF16),
            pltpu.VMEM((8, slots), F32),
            pltpu.VMEM((16, slots), BF16),
        ),
        in_specs=[hbm] * 5,
        out_specs=(vmem, vmem, vmem),
        scratch_shapes=[
            pltpu.SMEM((tiles,), jnp.int32),
            pltpu.VMEM((8, slots), F32),
            pltpu.VMEM((8, slots), F32),
            pltpu.VMEM((8, 2 * slots), F32),
        ] + [pltpu.SemaphoreType.DMA] * 5,
        name="pack",
    )(obs_count, obs, state, innovation, obs_precision)


def mm(a, b):
    return jnp.dot(a.astype(BF16), b.astype(BF16), preferred_element_type=F32)


C0, C1, C2, C3, C4 = 2.25, -2.4375, 1.6875, -0.5625, 0.0625


def analyse_kernel(got_ref, weight_ref, push_ref, out_ref, sum_ref):
    sources, blocks, each, _ = got_ref.shape
    members = sources * each
    width = (blocks - LIVE) // 2

    def values_of(block):
        return got_ref[:, block].reshape(members, BLOCK)

    def product(first, last, tiles):
        observed = [values_of(block) for block in range(first, last)]
        at = slice(first * BLOCK, last * BLOCK)
        rows = []
        for tile in tiles:
            rows.append(jnp.concatenate(
                [(x.astype(F32) * weight_ref[pl.ds(tile, 1), pl.ds((first + i) * BLOCK, BLOCK)]).astype(BF16)
                 for i, x in enumerate(observed)], axis=1))
        left = jnp.concatenate(rows + [push_ref[:, at]], axis=0)
        return lax.dot_general(
            left, jnp.concatenate(observed, axis=1), LAST, preferred_element_type=F32)

    stretch = lax.div(jnp.max(weight_ref[pl.ds(2, 1), :BLOCK]).astype(jnp.int32), STEP)
    for part in range(LIVE // STEP):
        low, high = part * STEP, (part + 1) * STEP

        @pl.when(stretch == part)
        def _():
            middle = product(low, high, (0, 1))
            first, second, lines = middle[:members], middle[members:2 * members], middle[2 * members:]
            if low:
                more = product(0, low, (0,))
                first, lines = first + more[:members], lines + more[members:]
            if high < LIVE:
                more = product(high, LIVE, (1,))
                second, lines = second + more[:members], lines + more[members:]
            sum_ref[:members] = first
            sum_ref[members:2 * members] = second
            sum_ref[2 * members:] = lines

    drives = sum_ref[2 * members:]
    drive = [jnp.sum(drives[3 * t:3 * t + 3], axis=0, keepdims=True) for t in range(2)]

    averages, deviations = [[], []], [[], []]
    waiting = [(t, q) for t in range(2) for q in range(width)]

    def prepare(count):
        for t, q in waiting[:count]:
            state = values_of(LIVE + t * width + q).astype(F32)
            average = jnp.sum(state, axis=0, keepdims=True) * (1.0 / members)
            averages[t].append(average)
            deviations[t].append((state - average).astype(BF16))
        del waiting[:count]

    on_diagonal = (lax.broadcasted_iota(jnp.int32, (members, members), 0)
                   == lax.broadcasted_iota(jnp.int32, (members, members), 1))
    unit, square, frob = [], [], []
    for t in range(2):
        system = sum_ref[t * members:(t + 1) * members]
        system = jnp.where(on_diagonal, system + (members - 1.0), system)
        raw = mm(system, system)
        norm = jnp.sqrt(jnp.sum(system * system, keepdims=True) + 1e-06)
        inverse = 1.0 / norm
        frob.append(norm)
        unit.append(system * inverse)
        square.append(raw * (inverse * inverse))
    prepare(2)

    def sweeps(e, square):
        tail = [mm(C3 * x + C4 * q, q) for q, x in zip(square, e)]
        return [C1 * x + C2 * q + r for x, q, r in zip(e, square, tail)]

    first = sweeps(unit, square)
    prepare(2)
    moved_y = [C0 * x + mm(d, x) for x, d in zip(unit, first)]
    prepare(2)
    error = [C0 * y + mm(y, d) for y, d in zip(moved_y, first)]
    prepare(2)
    second = sweeps(error, [mm(x, x) for x in error])
    rest = [C0 * (d + q) + mm(q, d) for d, q in zip(first, second)]

    for t in range(2):
        root = jnp.where(on_diagonal, rest[t] + C0 * C0, rest[t])
        once = jnp.sum(root * drive[t], axis=1, keepdims=True)
        shift = jnp.sum(root * once, axis=0, keepdims=True) / frob[t]
        scale = jnp.sqrt((members - 1.0) / frob[t])
        transform = (shift + root * scale).astype(BF16)
        moved = mm(transform, jnp.concatenate(deviations[t], axis=1))
        for q in range(width):
            result = averages[t][q] + moved[:, q * BLOCK:(q + 1) * BLOCK]
            out_ref[:, t * width + q] = result.astype(BF16).reshape(sources, each, BLOCK)


def analyse(got, weights, pushes):
    sources, blocks, each, _ = got.shape
    members = sources * each
    vmem = pl.BlockSpec(memory_space=pltpu.VMEM)
    here = lambda x: pltpu.with_memory_space_constraint(x, pltpu.VMEM)
    return pl.pallas_call(
        analyse_kernel,
        out_shape=pltpu.VMEM((sources, blocks - LIVE, each, BLOCK), BF16),
        in_specs=[vmem, vmem, vmem],
        out_specs=vmem,
        scratch_shapes=[pltpu.VMEM((2 * members + 16, members), F32)],
        name="analyse",
    )(here(got), here(weights), here(pushes))


def local(ens_obs, ens_state, innovation, obs_precision, obs_count):
    tiles, each, variables = ens_state.shape
    exchange = lambda x: lax.all_to_all(x, "member", split_axis=0, concat_axis=0, tiled=True)
    packed, weights, pushes = pack(obs_count, ens_obs, ens_state, innovation, obs_precision)
    back = exchange(analyse(exchange(packed), weights, pushes))
    back = back.reshape(tiles, variables // BLOCK, each, BLOCK)
    return back.transpose(0, 2, 1, 3).reshape(tiles, each, variables)


def solution(mesh):
    placed = (
        P("region", "member", None),
        P("region", "member", None),
        P("region", None),
        P("region", None),
        P("region"),
    )
    return jax.shard_map(
        local, mesh=mesh, in_specs=placed, out_specs=P("region", "member", None), check_vma=False
    )
```
